256 devices in a mesh: ka: 32 (over z_lo, y, core), pa: 8 (over z_hi, x).
Axes of the slice: x: 4, y: 4, z: 8 (z_hi: 2, z_lo: 4; z = z_hi * 4 + z_lo), core: 2. Of those that a mesh axis runs over, the one named last changes fastest.
Arguments:
- previous: float32 [256, 256, 256], P('ka', None, 'pa'), may hold values from -6 to 6
- current: float32 [256, 256, 256], P('ka', None, 'pa'), may hold values from -6 to 6
- energies: float32 [256, 256, 256], P('ka', None, 'pa'), may hold values from -0.5 to 0.5
- valence: float32 [256, 256, 256], P('ka'), may hold values from -0.375 to 0.375
- conduction: float32 [256, 256, 256], P('ka', None, 'pa'), may hold values from -0.375 to 0.375
- kernel: float32 [256, 256, 256], P(None, 'ka', 'pa'), may hold values from 0.05 to 0.35
Outputs:
- next_one: float32 [256, 256, 256], P('ka', None, 'pa')
- next_two: float32 [256, 256, 256], P('ka', None, 'pa')
The draws below stay inside these ranges and needn't reach their ends.
All inputs are finite; a program needn't handle non-finite values.
Results may differ from the reference program's by a relative error of at most 0.000096.
Values sent between devices are 32-bit elements; how exact they have to be, the bound alone decides.
No kernel may reach another device: no remote copies, remote signals or barrier semaphores. Data moves between devices by JAX's collectives and lax.ppermute only.
A program may use at most 64 MiB of HBM per device.

```python
import math
import jax
import jax.numpy as jnp
from jax import lax

V = 256
C = 256
P_SIZE = 256
KY = 16
NK = 256


def block_levels(stream_key, dims, shards, low, largest):
    loudness = 1.0
    for dim, parts in shards:
        steps = jax.random.uniform(jax.random.fold_in(jax.random.fold_in(stream_key, 6), dim), (parts,), jnp.float32, low / len(shards), largest / len(shards))
        loudness = loudness * jnp.repeat(jnp.exp(steps), dims[dim] // parts).reshape((-1,) + (1,) * (len(dims) - 1 - dim))
    return loudness


def scatter_about(stream_key, dims, deviation, reach, split=(), dtype=jnp.bfloat16):
    array = deviation * jax.random.normal(stream_key, dims, jnp.float32)
    if split:
        array = array * block_levels(stream_key, dims, split, -0.22, 0.18)
    return jnp.clip(array, -reach, reach).astype(dtype)


def setup_inputs(seed: int = 0) -> dict:
    arg_keys = jax.random.split(jax.random.key(seed), 7)
    previous = scatter_about(arg_keys[0], (NK, V, C), 1.0, 6.0, ((0, 32), (2, 8)), jnp.float32)
    current = scatter_about(arg_keys[1], (NK, V, C), 1.0, 6.0, ((0, 32), (2, 8)), jnp.float32)
    energies = jnp.clip(jax.random.uniform(arg_keys[2], (NK, V, C), jnp.float32, -0.5, 0.5) * block_levels(arg_keys[2], (NK, V, C), ((0, 32), (2, 8)), -0.4, 0.0), -0.5, 0.5)
    valence = scatter_about(arg_keys[3], (NK, V, P_SIZE), V ** -0.5, 0.375, ((0, 32),), jnp.float32)
    conduction = scatter_about(arg_keys[4], (NK, C, P_SIZE), C ** -0.5, 0.375, ((0, 32), (2, 8)), jnp.float32)
    kernel = jnp.clip(0.05 + 0.29999999 * jax.random.uniform(arg_keys[5], (NK, P_SIZE, P_SIZE), jnp.float32) ** block_levels(arg_keys[5], (NK, P_SIZE, P_SIZE), ((1, 32), (2, 8)), -0.2, 0.2), 0.05, 0.35)
    return {"previous": previous, "current": current, "energies": energies, "valence": valence, "conduction": conduction, "kernel": kernel}


def phase_tables(total):
    points = jnp.arange(total)
    wide = total // KY
    coarse = points // KY
    finer = points % KY
    turns = ((coarse[:, None] * coarse[None, :]) % wide).astype(jnp.float32) / wide
    turns = turns + ((finer[:, None] * finer[None, :]) % KY).astype(jnp.float32) / KY
    angles = 2.0 * math.pi * turns
    return jnp.cos(angles), jnp.sin(angles)


def kernel_product(field, valence, conduction, kernel, cosine_table, sine_table):
    total = field.shape[0]
    width = valence.shape[2]
    highest = lax.Precision.HIGHEST
    inner = jnp.einsum("kvc,kcn->kvn", field, conduction, precision=highest)
    pair_blocks = jnp.einsum("kvm,kvn->kmn", valence, inner, precision=highest)
    flattened = pair_blocks.reshape(total, width * width)
    even = jnp.dot(cosine_table, flattened, precision=highest)
    odd = jnp.dot(sine_table, flattened, precision=highest)
    weights = kernel.reshape(total, width * width)
    screened = (jnp.dot(cosine_table, weights * even, precision=highest) + jnp.dot(sine_table, weights * odd, precision=highest)) / total
    screened = screened.reshape(total, width, width)
    partial_rows = jnp.einsum("kmn,kcn->kmc", screened, conduction, precision=highest)
    return jnp.einsum("kvm,kmc->kvc", valence, partial_rows, precision=highest)


def reference(previous, current, energies, valence, conduction, kernel):
    cosine_table, sine_table = phase_tables(current.shape[0])
    first = energies * current + kernel_product(current, valence, conduction, kernel, cosine_table, sine_table)
    next_one = 2.0 * first - previous
    second = energies * next_one + kernel_product(next_one, valence, conduction, kernel, cosine_table, sine_table)
    next_two = 2.0 * second - current
    return next_one, next_two
```

```python
import math

import jax
import jax.numpy as jnp
import numpy as np
from jax import lax
from jax.sharding import PartitionSpec as P

KY = 16
HIGHEST = lax.Precision.HIGHEST


def real_transform(total):
    wide = total // KY
    points = np.arange(total)
    coarse, finer = points // KY, points % KY
    mirror = (-coarse % wide) * KY + (-finer % KY)
    alone = [q for q in range(total) if mirror[q] == q]
    paired = [q for q in range(total) if q < mirror[q]]
    turns = (coarse[:, None] * coarse[None, :] % wide) / wide
    turns = turns + (finer[:, None] * finer[None, :] % KY) / KY
    angles = 2.0 * math.pi * turns
    cosine, sine = np.cos(angles), np.sin(angles)
    rows = np.concatenate([cosine[alone], cosine[paired], sine[paired]])
    pick = np.zeros((total, total))
    for i, q in enumerate(alone + paired + paired):
        pick[i, q] = 1.0
        pick[i, mirror[q]] = 1.0
    return rows.astype(np.float32), pick.astype(np.float32)


def product(a, b, dims):
    return lax.dot_general(a, b, (dims, ((), ())), precision=HIGHEST)


def on_device(previous, current, energies, valence, conduction, kernel):
    total = kernel.shape[0]
    rows, pick = real_transform(total)
    both = ("ka", "pa")
    current_t = jnp.swapaxes(current, 1, 2)
    base_t = 2.0 * jnp.swapaxes(energies, 1, 2) * current_t - jnp.swapaxes(previous, 1, 2)
    conduction_t = jnp.swapaxes(conduction, 1, 2)
    kernel_t = jnp.transpose(kernel, (1, 2, 0))
    per_k, slim, bands = current_t.shape
    packed = jnp.stack([current_t, conduction_t, base_t, kernel_t], axis=1)
    packed = lax.all_to_all(packed, "pa", split_axis=0, concat_axis=0, tiled=True)
    whole = [packed[:, i].reshape(per_k * slim, bands) for i in range(4)]
    field_t, conduct_t, whole_base_t, weights_t = whole
    val = lax.dynamic_index_in_dim(valence, lax.axis_index("pa"), 0, keepdims=False)
    weights = product(pick, weights_t, ((1,), (1,))) / total

    def exchange(block):
        block = block.reshape(total, 1, block.shape[1])
        block = lax.all_to_all(block, both, split_axis=0, concat_axis=0, tiled=True)
        return block.reshape(total, block.shape[2])

    def applied_t(amplitudes_t):
        inner = product(conduct_t, amplitudes_t, ((1,), (0,)))
        pairs = product(val, inner, ((0,), (1,)))
        owned = exchange(pairs)
        modes = product(rows, owned, ((1,), (0,))) * weights
        screened = exchange(product(rows, modes, ((0,), (0,))))
        partial = product(conduct_t, screened, ((0,), (1,)))
        return product(partial, val, ((1,), (1,)))

    next_t = whole_base_t + 2.0 * applied_t(field_t)
    second_t = applied_t(next_t)
    home = jnp.stack([next_t, second_t]).reshape(2, per_k, slim, bands)
    home = lax.all_to_all(jnp.swapaxes(home, 0, 1), "pa", split_axis=0, concat_axis=0, tiled=True)
    next_one = jnp.swapaxes(home[:, 0], 1, 2)
    second = jnp.swapaxes(home[:, 1], 1, 2)
    next_two = 2.0 * (energies * next_one + second) - current
    return next_one, next_two


def solution(mesh):
    banded = P("ka", None, "pa")
    return jax.shard_map(
        on_device,
        mesh=mesh,
        in_specs=(banded, banded, banded, P("ka", None, None), banded, P(None, "ka", "pa")),
        out_specs=(banded, banded),
        check_vma=False,
    )
```

```python
import math

import jax
import jax.numpy as jnp
import numpy as np
from jax import lax
from jax.experimental import pallas as pl
from jax.experimental.pallas import tpu as pltpu
from jax.sharding import PartitionSpec as P

KY = 16
LANES = 128
VMEM_BYTES = 16 * 1024 * 1024
F32 = jnp.float32
BF16 = jnp.bfloat16
NN = (((1,), (0,)), ((), ()))
NT = (((1,), (1,)), ((), ()))


def real_transform(total):
    wide = total // KY
    points = np.arange(total)
    coarse, finer = points // KY, points % KY
    mirror = (-coarse % wide) * KY + (-finer % KY)
    alone = [q for q in range(total) if mirror[q] == q]
    paired = [q for q in range(total) if q < mirror[q]]
    turns = (coarse[:, None] * coarse[None, :] % wide) / wide
    turns = turns + (finer[:, None] * finer[None, :] % KY) / KY
    angles = 2.0 * math.pi * turns
    cosine, sine = np.cos(angles), np.sin(angles)
    rows = np.concatenate([cosine[alone], cosine[paired], sine[paired]])
    pick = np.zeros((total, total))
    for i, q in enumerate(alone + paired + paired):
        pick[i, q] = 1.0
        pick[i, mirror[q]] = 1.0
    return rows.astype(np.float32), pick.astype(np.float32)


def split_table(table):
    high = table.astype(BF16)
    return high, (table - high.astype(np.float32)).astype(BF16)


def split(x):
    high = x.astype(BF16)
    return high, (x - high.astype(F32)).astype(BF16)


def dot3(a, b, dims=NN):
    one = lambda p, q: lax.dot_general(p, q, dims, preferred_element_type=F32)
    return one(a[0], b[0]) + (one(a[0], b[1]) + one(a[1], b[0]))


def swap_groups(blocks):
    lane = lax.broadcasted_iota(jnp.int32, blocks[0].shape, 1)
    low = lane < 64
    a, b, c, d = blocks
    turn = lambda x, by: pltpu.roll(x, by, 1)
    a, c = jnp.where(low, a, turn(c, 64)), jnp.where(low, turn(a, 64), c)
    b, d = jnp.where(low, b, turn(d, 64)), jnp.where(low, turn(b, 64), d)
    even = (lane // 32) % 2 == 0
    a, b = jnp.where(even, a, turn(b, 32)), jnp.where(even, turn(a, 96), b)
    c, d = jnp.where(even, c, turn(d, 32)), jnp.where(even, turn(c, 96), d)
    return a, b, c, d


def store_messages(pairs, out_ref):
    for half in range(2):
        for part in range(2):
            blocks = [pairs[(4 * part + i) * 32 : (4 * part + i) * 32 + 32, half * LANES : (half + 1) * LANES] for i in range(4)]
            for p, block in enumerate(swap_groups(blocks)):
                out_ref[pl.ds((half * 4 + p) * 2 + part, 32, stride=16), :] = block


def load_messages(in_ref):
    halves = []
    for half in range(2):
        rows = []
        for part in range(2):
            blocks = [in_ref[pl.ds((half * 4 + p) * 2 + part, 32, stride=16), :] for p in range(4)]
            rows.extend(swap_groups(blocks))
        halves.append(jnp.concatenate(rows, axis=0))
    return jnp.concatenate(halves, axis=1)


def pack_kernel(previous_ref, current_ref, energies_ref, conduction_ref, out_ref):
    current = current_ref[...]
    out_ref[:, 0] = current
    out_ref[:, 1] = conduction_ref[...]
    out_ref[:, 2] = 2.0 * energies_ref[...] * current - previous_ref[...]


def valence_kernel(index_ref, valence_ref, high_ref, low_ref, turned_ref):
    del index_ref
    turned = valence_ref[0].T
    for half in range(2):
        columns = slice(half * LANES, (half + 1) * LANES)
        turned_ref[half] = turned[:, columns]
        for row in range(8):
            high, low = split(turned_ref[half, pl.ds(row, 32, stride=8), :])
            high_ref[row * 32 : row * 32 + 32, columns] = high
            low_ref[row * 32 : row * 32 + 32, columns] = low


def square(ref, which):
    block = ref[:, which]
    return block.reshape(block.shape[0] * block.shape[1], block.shape[2])


def first_pairs_kernel(whole_ref, high_ref, low_ref, out_ref):
    conduct = split(square(whole_ref, 1))
    inner = dot3(conduct, split(square(whole_ref, 0)))
    store_messages(dot3((high_ref[...], low_ref[...]), split(inner), NT), out_ref)


def screen_kernel(owned_ref, rows_high, rows_low, back_high, back_low, weights_ref, out_ref):
    total = weights_ref.shape[0]
    owned = jnp.concatenate([owned_ref[pl.ds(part, total, stride=2), :] for part in range(2)], axis=1)
    modes = dot3((rows_high[...], rows_low[...]), split(owned)) * weights_ref[...]
    screened = dot3((back_high[...], back_low[...]), split(modes))
    for part in range(2):
        out_ref[pl.ds(part, total, stride=2), :] = screened[:, part * LANES : (part + 1) * LANES]


def product_back(screened_ref, conduct, valence):
    partial = dot3(split(load_messages(screened_ref)), conduct)
    return dot3(split(partial.T), valence)


def next_pairs_kernel(screened_ref, whole_ref, high_ref, low_ref, next_ref, out_ref):
    conduct = split(square(whole_ref, 1))
    valence = high_ref[...], low_ref[...]
    following = square(whole_ref, 2) + 2.0 * product_back(screened_ref, conduct, valence)
    next_ref[...] = following
    inner = dot3(conduct, split(following))
    store_messages(dot3(valence, split(inner), NT), out_ref)


def last_kernel(screened_ref, whole_ref, high_ref, low_ref, next_ref, out_ref):
    conduct = split(square(whole_ref, 1))
    second = product_back(screened_ref, conduct, (high_ref[...], low_ref[...]))
    shape = out_ref.shape[0], out_ref.shape[2], out_ref.shape[3]
    out_ref[:, 0] = next_ref[...].reshape(shape)
    out_ref[:, 1] = second.reshape(shape)


def call(kernel, outs, flops, moved, **more):
    return pl.pallas_call(
        kernel,
        out_shape=outs,
        compiler_params=pltpu.CompilerParams(vmem_limit_bytes=VMEM_BYTES),
        cost_estimate=pl.CostEstimate(flops=flops, bytes_accessed=moved, transcendentals=0),
        **more,
    )


def on_device(previous, current, energies, valence, conduction, kernel):
    total = kernel.shape[0]
    rows, pick = real_transform(total)
    both = ("ka", "pa")
    banded = lambda x: jnp.swapaxes(x, 1, 2)
    per_k, bands, slim = current.shape
    flops = 2 * total**3
    size = 4 * total**2
    shaped = jax.ShapeDtypeStruct
    tables = [jnp.asarray(t) for t in (*split_table(rows), *split_table(rows.T.copy()))]

    packed = call(pack_kernel, shaped((per_k, 3, slim, bands), F32), 3 * total**2, 7 * size)(
        banded(previous), banded(current), banded(energies), banded(conduction)
    )
    whole = lax.all_to_all(packed, "pa", split_axis=0, concat_axis=0, tiled=True)

    high, low = call(
        valence_kernel,
        [shaped((total, bands), BF16)] * 2,
        total**2,
        2 * size,
        grid_spec=pltpu.PrefetchScalarGridSpec(
            num_scalar_prefetch=1,
            grid=(1,),
            in_specs=[pl.BlockSpec((1, bands, total), lambda i, index: (index[0], 0, 0))],
            out_specs=[pl.BlockSpec((total, bands), lambda i, index: (0, 0))] * 2,
            scratch_shapes=[pltpu.VMEM((2, total, LANES), F32)],
        ),
    )(lax.axis_index("pa").reshape(1), valence)
    kernel_t = jnp.transpose(kernel, (1, 2, 0)).reshape(total, total)
    weights = lax.dot_general(pick, kernel_t, NT, precision=lax.Precision.HIGHEST) / total

    def exchange(block):
        block = block.reshape(total, 2, LANES)
        block = lax.all_to_all(block, both, split_axis=0, concat_axis=0, tiled=True)
        return block.reshape(2 * total, LANES)

    message = shaped((2 * total, LANES), F32)
    screen = call(screen_kernel, message, 6 * flops, 5 * size)

    pairs = call(first_pairs_kernel, message, 6 * flops, 4 * size)(whole, high, low)
    back = exchange(screen(exchange(pairs), *tables, weights))
    following, pairs = call(next_pairs_kernel, [shaped((total, bands), F32), message], 12 * flops, 6 * size)(
        back, whole, high, low
    )
    back = exchange(screen(exchange(pairs), *tables, weights))
    home = call(last_kernel, shaped((per_k, 2, slim, bands), F32), 6 * flops, 6 * size)(
        back, whole, high, low, following
    )
    home = lax.all_to_all(home, "pa", split_axis=0, concat_axis=0, tiled=True)
    next_one = banded(home[:, 0])
    next_two = 2.0 * (energies * next_one + banded(home[:, 1])) - current
    return next_one, next_two


def solution(mesh):
    banded = P("ka", None, "pa")
    return jax.shard_map(
        on_device,
        mesh=mesh,
        in_specs=(banded, banded, banded, P("ka", None, None), banded, P(None, "ka", "pa")),
        out_specs=(banded, banded),
        check_vma=False,
    )
```

```python
import math

import jax
import jax.numpy as jnp
import numpy as np
from jax import lax
from jax.experimental import pallas as pl
from jax.experimental.pallas import tpu as pltpu
from jax.sharding import PartitionSpec as P

KY = 16
LANES = 128
VMEM_BYTES = 16 * 1024 * 1024
F32 = jnp.float32
BF16 = jnp.bfloat16
NN = (((1,), (0,)), ((), ()))
NT = (((1,), (1,)), ((), ()))


def real_transform(total):
    wide = total // KY
    points = np.arange(total)
    coarse, finer = points // KY, points % KY
    mirror = (-coarse % wide) * KY + (-finer % KY)
    alone = [q for q in range(total) if mirror[q] == q]
    paired = [q for q in range(total) if q < mirror[q]]
    turns = (coarse[:, None] * coarse[None, :] % wide) / wide
    turns = turns + (finer[:, None] * finer[None, :] % KY) / KY
    angles = 2.0 * math.pi * turns
    cosine, sine = np.cos(angles), np.sin(angles)
    rows = np.concatenate([cosine[alone], cosine[paired], sine[paired]])
    pick = np.zeros((total, total))
    for i, q in enumerate(alone + paired + paired):
        pick[i, q] = 1.0
        pick[i, mirror[q]] = 1.0
    return rows.astype(np.float32), pick.astype(np.float32)


def split_table(table):
    high = table.astype(BF16)
    return high, (table - high.astype(np.float32)).astype(BF16)


def split(x):
    high = x.astype(BF16)
    return high, (x - high.astype(F32)).astype(BF16)


def dot3(a, b, dims=NN):
    one = lambda p, q: lax.dot_general(p, q, dims, preferred_element_type=F32)
    return one(a[0], b[0]) + (one(a[0], b[1]) + one(a[1], b[0]))


def swap_groups(blocks):
    lane = lax.broadcasted_iota(jnp.int32, blocks[0].shape, 1)
    low = lane < 64
    a, b, c, d = blocks
    turn = lambda x, by: pltpu.roll(x, by, 1)
    a, c = jnp.where(low, a, turn(c, 64)), jnp.where(low, turn(a, 64), c)
    b, d = jnp.where(low, b, turn(d, 64)), jnp.where(low, turn(b, 64), d)
    even = (lane // 32) % 2 == 0
    a, b = jnp.where(even, a, turn(b, 32)), jnp.where(even, turn(a, 96), b)
    c, d = jnp.where(even, c, turn(d, 32)), jnp.where(even, turn(c, 96), d)
    return a, b, c, d


def store_messages(pairs, out_ref):
    for half in range(2):
        for part in range(2):
            blocks = [pairs[(4 * part + i) * 32 : (4 * part + i) * 32 + 32, half * LANES : (half + 1) * LANES] for i in range(4)]
            for p, block in enumerate(swap_groups(blocks)):
                out_ref[pl.ds((half * 4 + p) * 2 + part, 32, stride=16), :] = block


def load_messages(in_ref):
    halves = []
    for half in range(2):
        rows = []
        for part in range(2):
            blocks = [in_ref[pl.ds((half * 4 + p) * 2 + part, 32, stride=16), :] for p in range(4)]
            rows.extend(swap_groups(blocks))
        halves.append(jnp.concatenate(rows, axis=0))
    return jnp.concatenate(halves, axis=1)


def pack_kernel(
    index_ref, previous_ref, current_ref, energies_ref, conduction_ref, valence_ref, out_ref, mine_ref, given, packed, arrived, left
):
    count = packed.shape[0]
    mine = pltpu.make_async_copy(valence_ref.at[index_ref[0]], mine_ref, left.at[count])

    def arrivals(k):
        pairs = (
            (current_ref, packed.at[k, 0]),
            (energies_ref, given.at[k, 0]),
            (previous_ref, given.at[k, 1]),
            (conduction_ref, packed.at[k, 1]),
        )
        return [pltpu.make_async_copy(ref.at[k], to, arrived.at[k, i]) for i, (ref, to) in enumerate(pairs)]

    def departure(k):
        return pltpu.make_async_copy(packed.at[k], out_ref.at[k], left.at[k])

    for k in range(count):
        for copy in arrivals(k):
            copy.start()
    mine.start()
    for k in range(count):
        for copy in arrivals(k):
            copy.wait()
        packed[k, 2] = 2.0 * given[k, 0] * packed[k, 0] - given[k, 1]
        departure(k).start()
    for k in range(count):
        departure(k).wait()
    mine.wait()


def prepare_kernel(mine_ref, kernel_ref, pick_ref, high_ref, low_ref, weights_ref, turned_ref):
    turned = mine_ref[...].T
    for half in range(2):
        columns = slice(half * LANES, (half + 1) * LANES)
        turned_ref[half] = turned[:, columns]
        for row in range(8):
            high, low = split(turned_ref[half, pl.ds(row, 32, stride=8), :])
            high_ref[row * 32 : row * 32 + 32, columns] = high
            low_ref[row * 32 : row * 32 + 32, columns] = low
    rest = kernel_ref[...]
    total = rest.shape[0]
    weights = jnp.zeros((total, total), F32)
    for _ in range(3):
        part = rest.astype(BF16)
        rest = rest - part.astype(F32)
        weights += lax.dot_general(pick_ref[...], part, NT, preferred_element_type=F32)
    weights_ref[...] = weights * (1.0 / total)


def square(ref, which):
    block = ref[:, which]
    return block.reshape(block.shape[0] * block.shape[1], block.shape[2])


def first_pairs_kernel(whole_ref, high_ref, low_ref, out_ref):
    conduct = split(square(whole_ref, 1))
    inner = dot3(conduct, split(square(whole_ref, 0)))
    store_messages(dot3((high_ref[...], low_ref[...]), split(inner), NT), out_ref)


def screen_kernel(owned_ref, rows_high, rows_low, back_high, back_low, weights_ref, out_ref):
    total = weights_ref.shape[0]
    owned = jnp.concatenate([owned_ref[pl.ds(part, total, stride=2), :] for part in range(2)], axis=1)
    modes = dot3((rows_high[...], rows_low[...]), split(owned)) * weights_ref[...]
    screened = dot3((back_high[...], back_low[...]), split(modes))
    for part in range(2):
        out_ref[pl.ds(part, total, stride=2), :] = screened[:, part * LANES : (part + 1) * LANES]


def product_back(screened_ref, conduct, valence):
    partial = dot3(split(load_messages(screened_ref)), conduct)
    return dot3(split(partial.T), valence)


def next_pairs_kernel(screened_ref, whole_ref, high_ref, low_ref, next_ref, out_ref):
    conduct = split(square(whole_ref, 1))
    valence = high_ref[...], low_ref[...]
    following = square(whole_ref, 2) + 2.0 * product_back(screened_ref, conduct, valence)
    next_ref[...] = following
    inner = dot3(conduct, split(following))
    store_messages(dot3(valence, split(inner), NT), out_ref)


def last_kernel(screened_ref, whole_ref, high_ref, low_ref, next_ref, out_ref):
    conduct = split(square(whole_ref, 1))
    second = product_back(screened_ref, conduct, (high_ref[...], low_ref[...]))
    shape = out_ref.shape[0], out_ref.shape[2], out_ref.shape[3]
    out_ref[:, 0] = next_ref[...].reshape(shape)
    out_ref[:, 1] = second.reshape(shape)


def call(kernel, outs, flops, moved, **more):
    return pl.pallas_call(
        kernel,
        out_shape=outs,
        compiler_params=pltpu.CompilerParams(vmem_limit_bytes=VMEM_BYTES),
        cost_estimate=pl.CostEstimate(flops=flops, bytes_accessed=moved, transcendentals=0),
        **more,
    )


def on_device(previous, current, energies, valence, conduction, kernel):
    total = kernel.shape[0]
    rows, pick = real_transform(total)
    both = ("ka", "pa")
    banded = lambda x: jnp.swapaxes(x, 1, 2)
    per_k, bands, slim = current.shape
    flops = 2 * total**3
    size = 4 * total**2
    shaped = jax.ShapeDtypeStruct
    tables = [jnp.asarray(t) for t in (*split_table(rows), *split_table(rows.T.copy()))]

    far = pl.BlockSpec(memory_space=pl.ANY)
    near = pl.BlockSpec(memory_space=pltpu.VMEM)
    packed, mine = pl.pallas_call(
        pack_kernel,
        out_shape=[shaped((per_k, 3, slim, bands), F32), shaped((bands, total), F32)],
        in_specs=[pl.BlockSpec(memory_space=pltpu.SMEM)] + [far] * 5,
        out_specs=[far, near],
        scratch_shapes=[
            pltpu.VMEM((per_k, 2, slim, bands), F32),
            pltpu.VMEM((per_k, 3, slim, bands), F32),
            pltpu.SemaphoreType.DMA((per_k, 4)),
            pltpu.SemaphoreType.DMA((per_k + 1,)),
        ],
        cost_estimate=pl.CostEstimate(flops=3 * total**2, bytes_accessed=8 * size, transcendentals=0),
    )(
        lax.axis_index("pa").reshape(1),
        banded(previous),
        banded(current),
        banded(energies),
        banded(conduction),
        valence,
    )
    whole = lax.all_to_all(packed, "pa", split_axis=0, concat_axis=0, tiled=True)

    high, low, weights = call(
        prepare_kernel,
        [shaped((total, bands), BF16)] * 2 + [shaped((total, total), F32)],
        3 * flops,
        5 * size,
        scratch_shapes=[pltpu.VMEM((2, total, LANES), F32)],
    )(mine, jnp.transpose(kernel, (1, 2, 0)).reshape(total, total), jnp.asarray(pick.astype(BF16)))

    def exchange(block):
        block = block.reshape(total, 2, LANES)
        block = lax.all_to_all(block, both, split_axis=0, concat_axis=0, tiled=True)
        return block.reshape(2 * total, LANES)

    message = shaped((2 * total, LANES), F32)
    screen = call(screen_kernel, message, 6 * flops, 5 * size)

    pairs = call(first_pairs_kernel, message, 6 * flops, 4 * size)(whole, high, low)
    back = exchange(screen(exchange(pairs), *tables, weights))
    following, pairs = call(next_pairs_kernel, [shaped((total, bands), F32), message], 12 * flops, 6 * size)(
        back, whole, high, low
    )
    back = exchange(screen(exchange(pairs), *tables, weights))
    home = call(last_kernel, shaped((per_k, 2, slim, bands), F32), 6 * flops, 6 * size)(
        back, whole, high, low, following
    )
    home = lax.all_to_all(home, "pa", split_axis=0, concat_axis=0, tiled=True)
    next_one = banded(home[:, 0])
    next_two = 2.0 * (energies * next_one + banded(home[:, 1])) - current
    return next_one, next_two


def solution(mesh):
    banded = P("ka", None, "pa")
    return jax.shard_map(
        on_device,
        mesh=mesh,
        in_specs=(banded, banded, banded, P("ka", None, None), banded, P(None, "ka", "pa")),
        out_specs=(banded, banded),
        check_vma=False,
    )
```

```python
import math

import jax
import jax.numpy as jnp
import numpy as np
from jax import lax
from jax.experimental import pallas as pl
from jax.experimental.pallas import tpu as pltpu
from jax.sharding import PartitionSpec as P

KY = 16
LANES = 128
VMEM_BYTES = 16 * 1024 * 1024
F32 = jnp.float32
BF16 = jnp.bfloat16
NN = (((1,), (0,)), ((), ()))
NT = (((1,), (1,)), ((), ()))


def real_transform(total):
    wide = total // KY
    points = np.arange(total)
    coarse, finer = points // KY, points % KY
    mirror = (-coarse % wide) * KY + (-finer % KY)
    alone = [q for q in range(total) if mirror[q] == q]
    paired = [q for q in range(total) if q < mirror[q]]
    turns = (coarse[:, None] * coarse[None, :] % wide) / wide
    turns = turns + (finer[:, None] * finer[None, :] % KY) / KY
    angles = 2.0 * math.pi * turns
    cosine, sine = np.cos(angles), np.sin(angles)
    rows = np.concatenate([cosine[alone], cosine[paired], sine[paired]])
    pick = np.zeros((total, total))
    for i, q in enumerate(alone + paired + paired):
        pick[i, q] = 1.0
        pick[i, mirror[q]] = 1.0
    return rows.astype(np.float32), pick.astype(np.float32)


def split_table(table):
    high = table.astype(BF16)
    return high, (table - high.astype(np.float32)).astype(BF16)


def split(x):
    high = x.astype(BF16)
    return high, (x - high.astype(F32)).astype(BF16)


def dot3(a, b, dims=NN):
    left = jnp.concatenate([a[0], a[0], a[1]], axis=1)
    right = jnp.concatenate([b[0], b[1], b[0]], axis=dims[0][1][0])
    return lax.dot_general(left, right, dims, preferred_element_type=F32)


def swap_groups(blocks):
    lane = lax.broadcasted_iota(jnp.int32, blocks[0].shape, 1)
    low = lane < 64
    a, b, c, d = blocks
    turn = lambda x, by: pltpu.roll(x, by, 1)
    a, c = jnp.where(low, a, turn(c, 64)), jnp.where(low, turn(a, 64), c)
    b, d = jnp.where(low, b, turn(d, 64)), jnp.where(low, turn(b, 64), d)
    even = (lane // 32) % 2 == 0
    a, b = jnp.where(even, a, turn(b, 32)), jnp.where(even, turn(a, 96), b)
    c, d = jnp.where(even, c, turn(d, 32)), jnp.where(even, turn(c, 96), d)
    return a, b, c, d


def store_messages(pairs, out_ref):
    for half in range(2):
        for part in range(2):
            blocks = [pairs[(4 * part + i) * 32 : (4 * part + i) * 32 + 32, half * LANES : (half + 1) * LANES] for i in range(4)]
            for p, block in enumerate(swap_groups(blocks)):
                out_ref[pl.ds((half * 4 + p) * 2 + part, 32, stride=16), :] = block


def load_messages(in_ref, part):
    halves = []
    for half in range(2):
        blocks = [in_ref[pl.ds((half * 4 + p) * 2 + part, 32, stride=16), :] for p in range(4)]
        halves.append(jnp.concatenate(swap_groups(blocks), axis=0))
    return jnp.concatenate(halves, axis=1)


def pack_kernel(
    index_ref,
    previous_ref,
    current_ref,
    energies_ref,
    conduction_ref,
    valence_ref,
    kernel_ref,
    pick_ref,
    packed_ref,
    high_ref,
    low_ref,
    weights_ref,
    given,
    mine,
    momenta,
    picked,
    turned,
    arrived,
    fixed,
):
    count = packed_ref.shape[0]
    copies = [
        pltpu.make_async_copy(ref, to, fixed.at[i])
        for i, (ref, to) in enumerate(
            ((valence_ref.at[index_ref[0]], mine), (kernel_ref, momenta), (pick_ref, picked))
        )
    ]

    def arrivals(k):
        pairs = (
            (current_ref, packed_ref.at[k, 0]),
            (energies_ref, given.at[k, 0]),
            (previous_ref, given.at[k, 1]),
            (conduction_ref, packed_ref.at[k, 1]),
        )
        return [pltpu.make_async_copy(ref.at[k], to, arrived.at[k, i]) for i, (ref, to) in enumerate(pairs)]

    for copy in copies:
        copy.start()
    for k in range(count):
        for copy in arrivals(k):
            copy.start()
    copies[0].wait()
    flipped = mine[...].T
    for half in range(2):
        columns = slice(half * LANES, (half + 1) * LANES)
        turned[half] = flipped[:, columns]
        for row in range(8):
            high, low = split(turned[half, pl.ds(row, 32, stride=8), :])
            high_ref[row * 32 : row * 32 + 32, columns] = high
            low_ref[row * 32 : row * 32 + 32, columns] = low
    copies[1].wait()
    copies[2].wait()
    rest = momenta[...]
    total = rest.shape[0]
    weights = jnp.zeros((total, total), F32)
    for _ in range(3):
        part = rest.astype(BF16)
        rest = rest - part.astype(F32)
        weights += lax.dot_general(picked[...], part, NT, preferred_element_type=F32)
    weights_ref[...] = weights * (1.0 / total)
    for k in range(count):
        for copy in arrivals(k):
            copy.wait()
        packed_ref[k, 2] = 2.0 * given[k, 0] * packed_ref[k, 0] - given[k, 1]


def square(ref, which):
    block = ref[:, which]
    return block.reshape(block.shape[0] * block.shape[1], block.shape[2])


def first_pairs_kernel(whole_ref, high_ref, low_ref, out_ref):
    conduct = split(square(whole_ref, 1))
    inner = dot3(conduct, split(square(whole_ref, 0)))
    store_messages(dot3((high_ref[...], low_ref[...]), split(inner), NT), out_ref)


def screen_kernel(owned_ref, rows_high, rows_low, back_high, back_low, weights_ref, out_ref):
    total = weights_ref.shape[0]
    owned = jnp.concatenate([owned_ref[pl.ds(part, total, stride=2), :] for part in range(2)], axis=1)
    modes = dot3((rows_high[...], rows_low[...]), split(owned)) * weights_ref[...]
    screened = dot3((back_high[...], back_low[...]), split(modes))
    for part in range(2):
        out_ref[pl.ds(part, total, stride=2), :] = screened[:, part * LANES : (part + 1) * LANES]


def product_back(screened_ref, conduct, valence):
    screened = jnp.concatenate([load_messages(screened_ref, part) for part in range(2)], axis=0)
    return dot3(split(dot3(conduct, split(screened), NT)), valence)


def product_back_by_halves(screened_ref, conduct, valence):
    total = 0.0
    for part in range(2):
        mine = slice(part * LANES, (part + 1) * LANES)
        partial = dot3(split(load_messages(screened_ref, part)), conduct)
        total += dot3(split(partial.T), (valence[0][mine], valence[1][mine]))
    return total


def next_pairs_kernel(screened_ref, whole_ref, high_ref, low_ref, next_ref, out_ref):
    conduct = split(square(whole_ref, 1))
    valence = high_ref[...], low_ref[...]
    following = square(whole_ref, 2) + 2.0 * product_back(screened_ref, split(square(whole_ref, 1).T), valence)
    next_ref[...] = following
    inner = dot3(conduct, split(following))
    store_messages(dot3(valence, split(inner), NT), out_ref)


def last_kernel(screened_ref, whole_ref, high_ref, low_ref, next_ref, out_ref):
    second = product_back_by_halves(screened_ref, split(square(whole_ref, 1)), (high_ref[...], low_ref[...]))
    shape = out_ref.shape[0], out_ref.shape[2], out_ref.shape[3]
    out_ref[:, 0] = next_ref[...].reshape(shape)
    out_ref[:, 1] = second.reshape(shape)


def call(kernel, outs, flops, moved, **more):
    return pl.pallas_call(
        kernel,
        out_shape=outs,
        compiler_params=pltpu.CompilerParams(vmem_limit_bytes=VMEM_BYTES),
        cost_estimate=pl.CostEstimate(flops=flops, bytes_accessed=moved, transcendentals=0),
        **more,
    )


def on_device(previous, current, energies, valence, conduction, kernel):
    total = kernel.shape[0]
    rows, pick = real_transform(total)
    both = ("ka", "pa")
    banded = lambda x: jnp.swapaxes(x, 1, 2)
    per_k, bands, slim = current.shape
    flops = 2 * total**3
    size = 4 * total**2
    shaped = jax.ShapeDtypeStruct
    tables = [jnp.asarray(t) for t in (*split_table(rows), *split_table(rows.T.copy()))]

    far = pl.BlockSpec(memory_space=pltpu.HBM)
    near = pl.BlockSpec(memory_space=pltpu.VMEM)
    packed, high, low, weights = pl.pallas_call(
        pack_kernel,
        out_shape=[shaped((per_k, 3, slim, bands), F32)]
        + [shaped((total, bands), BF16)] * 2
        + [shaped((total, total), F32)],
        in_specs=[pl.BlockSpec(memory_space=pltpu.SMEM)] + [far] * 7,
        out_specs=[near] * 4,
        scratch_shapes=[
            pltpu.VMEM((per_k, 2, slim, bands), F32),
            pltpu.VMEM((bands, total), F32),
            pltpu.VMEM((total, total), F32),
            pltpu.VMEM((total, total), BF16),
            pltpu.VMEM((2, total, LANES), F32),
            pltpu.SemaphoreType.DMA((per_k, 4)),
            pltpu.SemaphoreType.DMA((3,)),
        ],
        compiler_params=pltpu.CompilerParams(vmem_limit_bytes=VMEM_BYTES),
        cost_estimate=pl.CostEstimate(flops=3 * flops, bytes_accessed=12 * size, transcendentals=0),
    )(
        lax.axis_index("pa").reshape(1),
        *(
            pltpu.with_memory_space_constraint(x, pltpu.HBM)
            for x in (
                banded(previous),
                banded(current),
                banded(energies),
                banded(conduction),
                valence,
                jnp.transpose(kernel, (1, 2, 0)).reshape(total, total),
                jnp.asarray(pick.astype(BF16)),
            )
        ),
    )
    whole = lax.all_to_all(packed, "pa", split_axis=0, concat_axis=0, tiled=True)

    def exchange(block):
        block = block.reshape(total, 2, LANES)
        block = lax.all_to_all(block, both, split_axis=0, concat_axis=0, tiled=True)
        return block.reshape(2 * total, LANES)

    message = shaped((2 * total, LANES), F32)
    screen = call(screen_kernel, message, 6 * flops, 5 * size)

    pairs = call(first_pairs_kernel, message, 6 * flops, 4 * size)(whole, high, low)
    back = exchange(screen(exchange(pairs), *tables, weights))
    following, pairs = call(next_pairs_kernel, [shaped((total, bands), F32), message], 12 * flops, 6 * size)(
        back, whole, high, low
    )
    back = exchange(screen(exchange(pairs), *tables, weights))
    home = call(last_kernel, shaped((per_k, 2, slim, bands), F32), 6 * flops, 6 * size)(
        back, whole, high, low, following
    )
    home = lax.all_to_all(home, "pa", split_axis=0, concat_axis=0, tiled=True)
    next_one = banded(home[:, 0])
    next_two = 2.0 * (energies * next_one + banded(home[:, 1])) - current
    return next_one, next_two


def solution(mesh):
    banded = P("ka", None, "pa")
    return jax.shard_map(
        on_device,
        mesh=mesh,
        in_specs=(banded, banded, banded, P("ka", None, None), banded, P(None, "ka", "pa")),
        out_specs=(banded, banded),
        check_vma=False,
    )
```

```python
import math

import jax
import jax.numpy as jnp
import numpy as np
from jax import lax
from jax.experimental import pallas as pl
from jax.experimental.pallas import tpu as pltpu
from jax.sharding import PartitionSpec as P

KY = 16
LANES = 128
VMEM_BYTES = 16 * 1024 * 1024
F32 = jnp.float32
BF16 = jnp.bfloat16
NN = (((1,), (0,)), ((), ()))
NT = (((1,), (1,)), ((), ()))


def real_transform(total):
    wide = total // KY
    points = np.arange(total)
    coarse, finer = points // KY, points % KY
    mirror = (-coarse % wide) * KY + (-finer % KY)
    alone = [q for q in range(total) if mirror[q] == q]
    paired = [q for q in range(total) if q < mirror[q]]
    turns = (coarse[:, None] * coarse[None, :] % wide) / wide
    turns = turns + (finer[:, None] * finer[None, :] % KY) / KY
    angles = 2.0 * math.pi * turns
    cosine, sine = np.cos(angles), np.sin(angles)
    rows = np.concatenate([cosine[alone], cosine[paired], sine[paired]])
    pick = np.zeros((total, total))
    for i, q in enumerate(alone + paired + paired):
        pick[i, q] = 1.0
        pick[i, mirror[q]] = 1.0
    return rows.astype(np.float32), pick.astype(np.float32)


def split_table(table):
    high = table.astype(BF16)
    return high, (table - high.astype(np.float32)).astype(BF16)


def split(x):
    high = x.astype(BF16)
    return high, (x - high.astype(F32)).astype(BF16)


def dot3(a, b, dims=NN):
    left = jnp.concatenate([a[0], a[0], a[1]], axis=1)
    right = jnp.concatenate([b[0], b[1], b[0]], axis=dims[0][1][0])
    return lax.dot_general(left, right, dims, preferred_element_type=F32)


def swap_groups(blocks):
    lane = lax.broadcasted_iota(jnp.int32, blocks[0].shape, 1)
    low = lane < 64
    a, b, c, d = blocks
    turn = lambda x, by: pltpu.roll(x, by, 1)
    a, c = jnp.where(low, a, turn(c, 64)), jnp.where(low, turn(a, 64), c)
    b, d = jnp.where(low, b, turn(d, 64)), jnp.where(low, turn(b, 64), d)
    even = (lane // 32) % 2 == 0
    a, b = jnp.where(even, a, turn(b, 32)), jnp.where(even, turn(a, 96), b)
    c, d = jnp.where(even, c, turn(d, 32)), jnp.where(even, turn(c, 96), d)
    return a, b, c, d


def store_messages(pairs, out_ref):
    for half in range(2):
        for part in range(2):
            blocks = [pairs[(4 * part + i) * 32 : (4 * part + i) * 32 + 32, half * LANES : (half + 1) * LANES] for i in range(4)]
            for p, block in enumerate(swap_groups(blocks)):
                out_ref[pl.ds((half * 4 + p) * 2 + part, 32, stride=16), :] = block


def load_messages(in_ref, part):
    halves = []
    for half in range(2):
        blocks = [in_ref[pl.ds((half * 4 + p) * 2 + part, 32, stride=16), :] for p in range(4)]
        halves.append(jnp.concatenate(swap_groups(blocks), axis=0))
    return jnp.concatenate(halves, axis=1)


def pack_kernel(
    index_ref,
    previous_ref,
    current_ref,
    energies_ref,
    conduction_ref,
    valence_ref,
    kernel_ref,
    pick_ref,
    packed_ref,
    high_ref,
    low_ref,
    weights_ref,
    given,
    mine,
    momenta,
    picked,
    turned,
    arrived,
    fixed,
):
    fields = [
        pltpu.make_async_copy(ref, to, arrived.at[i])
        for i, (ref, to) in enumerate(
            (
                (current_ref, packed_ref.at[:, 0]),
                (energies_ref, given.at[0]),
                (previous_ref, given.at[1]),
                (conduction_ref, packed_ref.at[:, 1]),
            )
        )
    ]
    copies = [
        pltpu.make_async_copy(ref, to, fixed.at[i])
        for i, (ref, to) in enumerate(
            ((valence_ref.at[index_ref[0]], mine), (kernel_ref, momenta), (pick_ref, picked))
        )
    ]
    for copy in copies + fields:
        copy.start()
    copies[0].wait()
    flipped = mine[...].T
    for half in range(2):
        columns = slice(half * LANES, (half + 1) * LANES)
        turned[half] = flipped[:, columns]
        for row in range(8):
            high, low = split(turned[half, pl.ds(row, 32, stride=8), :])
            high_ref[row * 32 : row * 32 + 32, columns] = high
            low_ref[row * 32 : row * 32 + 32, columns] = low
    copies[1].wait()
    copies[2].wait()
    rest = momenta[...]
    total = rest.shape[0]
    weights = jnp.zeros((total, total), F32)
    for _ in range(3):
        part = rest.astype(BF16)
        rest = rest - part.astype(F32)
        weights += lax.dot_general(picked[...], part, NT, preferred_element_type=F32)
    weights_ref[...] = weights * (1.0 / total)
    for copy in fields:
        copy.wait()
    packed_ref[:, 2] = 2.0 * given[0] * packed_ref[:, 0] - given[1]


def square(ref, which):
    block = ref[:, which]
    return block.reshape(block.shape[0] * block.shape[1], block.shape[2])


def first_pairs_kernel(whole_ref, high_ref, low_ref, out_ref):
    conduct = split(square(whole_ref, 1))
    inner = dot3(conduct, split(square(whole_ref, 0)))
    store_messages(dot3((high_ref[...], low_ref[...]), split(inner), NT), out_ref)


def screen_kernel(owned_ref, rows_high, rows_low, back_high, back_low, weights_ref, out_ref):
    total = weights_ref.shape[0]
    owned = split(jnp.concatenate([owned_ref[pl.ds(part, total, stride=2), :] for part in range(2)], axis=1))
    screened = 0.0
    for part in range(2):
        mine = slice(part * LANES, (part + 1) * LANES)
        modes = dot3((rows_high[mine], rows_low[mine]), owned) * weights_ref[mine]
        screened += dot3((back_high[:, mine], back_low[:, mine]), split(modes))
    for part in range(2):
        out_ref[pl.ds(part, total, stride=2), :] = screened[:, part * LANES : (part + 1) * LANES]


def product_back(screened_ref, conduct, valence):
    screened = jnp.concatenate([load_messages(screened_ref, part) for part in range(2)], axis=0)
    return dot3(split(dot3(conduct, split(screened), NT)), valence)


def product_back_by_halves(screened_ref, conduct, valence):
    total = 0.0
    for part in range(2):
        mine = slice(part * LANES, (part + 1) * LANES)
        partial = dot3(split(load_messages(screened_ref, part)), conduct)
        total += dot3(split(partial.T), (valence[0][mine], valence[1][mine]))
    return total


def next_pairs_kernel(screened_ref, whole_ref, high_ref, low_ref, next_ref, out_ref):
    conduct = split(square(whole_ref, 1))
    valence = high_ref[...], low_ref[...]
    following = square(whole_ref, 2) + 2.0 * product_back(screened_ref, split(square(whole_ref, 1).T), valence)
    next_ref[...] = following
    inner = dot3(conduct, split(following))
    store_messages(dot3(valence, split(inner), NT), out_ref)


def last_kernel(screened_ref, whole_ref, high_ref, low_ref, next_ref, out_ref):
    second = product_back_by_halves(screened_ref, split(square(whole_ref, 1)), (high_ref[...], low_ref[...]))
    shape = out_ref.shape[0], out_ref.shape[2], out_ref.shape[3]
    out_ref[:, 0] = next_ref[...].reshape(shape)
    out_ref[:, 1] = second.reshape(shape)


def call(kernel, outs, flops, moved, **more):
    return pl.pallas_call(
        kernel,
        out_shape=outs,
        compiler_params=pltpu.CompilerParams(vmem_limit_bytes=VMEM_BYTES),
        cost_estimate=pl.CostEstimate(flops=flops, bytes_accessed=moved, transcendentals=0),
        **more,
    )


def on_device(previous, current, energies, valence, conduction, kernel):
    total = kernel.shape[0]
    rows, pick = real_transform(total)
    both = ("ka", "pa")
    banded = lambda x: jnp.swapaxes(x, 1, 2)
    per_k, bands, slim = current.shape
    flops = 2 * total**3
    size = 4 * total**2
    shaped = jax.ShapeDtypeStruct
    tables = [jnp.asarray(t) for t in (*split_table(rows), *split_table(rows.T.copy()))]

    far = pl.BlockSpec(memory_space=pltpu.HBM)
    near = pl.BlockSpec(memory_space=pltpu.VMEM)
    packed, high, low, weights = pl.pallas_call(
        pack_kernel,
        out_shape=[shaped((per_k, 3, slim, bands), F32)]
        + [shaped((total, bands), BF16)] * 2
        + [shaped((total, total), F32)],
        in_specs=[pl.BlockSpec(memory_space=pltpu.SMEM)] + [far] * 7,
        out_specs=[near] * 4,
        scratch_shapes=[
            pltpu.VMEM((2, per_k, slim, bands), F32),
            pltpu.VMEM((bands, total), F32),
            pltpu.VMEM((total, total), F32),
            pltpu.VMEM((total, total), BF16),
            pltpu.VMEM((2, total, LANES), F32),
            pltpu.SemaphoreType.DMA((4,)),
            pltpu.SemaphoreType.DMA((3,)),
        ],
        compiler_params=pltpu.CompilerParams(vmem_limit_bytes=VMEM_BYTES),
        cost_estimate=pl.CostEstimate(flops=3 * flops, bytes_accessed=12 * size, transcendentals=0),
    )(
        lax.axis_index("pa").reshape(1),
        *(
            pltpu.with_memory_space_constraint(x, pltpu.HBM)
            for x in (
                banded(previous),
                banded(current),
                banded(energies),
                banded(conduction),
                valence,
                jnp.transpose(kernel, (1, 2, 0)).reshape(total, total),
                jnp.asarray(pick.astype(BF16)),
            )
        ),
    )
    whole = lax.all_to_all(packed, "pa", split_axis=0, concat_axis=0, tiled=True)

    def exchange(block):
        block = block.reshape(total, 2, LANES)
        block = lax.all_to_all(block, both, split_axis=0, concat_axis=0, tiled=True)
        return block.reshape(2 * total, LANES)

    message = shaped((2 * total, LANES), F32)
    screen = call(screen_kernel, message, 6 * flops, 5 * size)

    pairs = call(first_pairs_kernel, message, 6 * flops, 4 * size)(whole, high, low)
    back = exchange(screen(exchange(pairs), *tables, weights))
    following, pairs = call(next_pairs_kernel, [shaped((total, bands), F32), message], 12 * flops, 6 * size)(
        back, whole, high, low
    )
    back = exchange(screen(exchange(pairs), *tables, weights))
    home = call(last_kernel, shaped((per_k, 2, slim, bands), F32), 6 * flops, 6 * size)(
        back, whole, high, low, following
    )
    home = lax.all_to_all(home, "pa", split_axis=0, concat_axis=0, tiled=True)
    next_one = banded(home[:, 0])
    next_two = 2.0 * (energies * next_one + banded(home[:, 1])) - current
    return next_one, next_two


def solution(mesh):
    banded = P("ka", None, "pa")
    return jax.shard_map(
        on_device,
        mesh=mesh,
        in_specs=(banded, banded, banded, P("ka", None, None), banded, P(None, "ka", "pa")),
        out_specs=(banded, banded),
        check_vma=False,
    )
```

```python
import math

import jax
import jax.numpy as jnp
import numpy as np
from jax import lax
from jax.experimental import pallas as pl
from jax.experimental.pallas import tpu as pltpu
from jax.sharding import PartitionSpec as P

KY = 16
LANES = 128
VMEM_BYTES = 16 * 1024 * 1024
F32 = jnp.float32
BF16 = jnp.bfloat16
NN = (((1,), (0,)), ((), ()))
NT = (((1,), (1,)), ((), ()))


def real_transform(total):
    wide = total // KY
    points = np.arange(total)
    coarse, finer = points // KY, points % KY
    mirror = (-coarse % wide) * KY + (-finer % KY)
    alone = [q for q in range(total) if mirror[q] == q]
    paired = [q for q in range(total) if q < mirror[q]]
    turns = (coarse[:, None] * coarse[None, :] % wide) / wide
    turns = turns + (finer[:, None] * finer[None, :] % KY) / KY
    angles = 2.0 * math.pi * turns
    cosine, sine = np.cos(angles), np.sin(angles)
    rows = np.concatenate([cosine[alone], cosine[paired], sine[paired]])
    pick = np.zeros((total, total))
    for i, q in enumerate(alone + paired + paired):
        pick[i, q] = 1.0
        pick[i, mirror[q]] = 1.0
    return rows.astype(np.float32), pick.astype(np.float32)


def split_table(table):
    high = table.astype(BF16)
    return high, (table - high.astype(np.float32)).astype(BF16)


def split(x):
    high = x.astype(BF16)
    return high, (x - high.astype(F32)).astype(BF16)


def dot3(a, b, dims=NN):
    left = jnp.concatenate([a[0], a[0], a[1]], axis=1)
    right = jnp.concatenate([b[0], b[1], b[0]], axis=dims[0][1][0])
    return lax.dot_general(left, right, dims, preferred_element_type=F32)


def choose(blocks, which):
    group = lax.broadcasted_iota(jnp.int32, blocks[0].shape, 1) // 32
    chosen = [blocks[(g - which) % 4] for g in range(4)]
    low = jnp.where(group == 0, chosen[0], chosen[1])
    high = jnp.where(group == 2, chosen[2], chosen[3])
    return jnp.where(group < 2, low, high)


def store_messages(pairs, out_ref):
    for half in range(2):
        for part in range(2):
            blocks = []
            for i in range(4):
                start = (4 * part + i) * 32
                block = pairs[start : start + 32, half * LANES : (half + 1) * LANES]
                blocks.append(pltpu.roll(block, 32 * i, 1) if i else block)
            for p in range(4):
                out_ref[pl.ds((half * 4 + p) * 2 + part, 32, stride=16), :] = choose(blocks, p)


def load_messages(in_ref, part):
    halves = []
    for half in range(2):
        blocks = [in_ref[pl.ds((half * 4 + p) * 2 + part, 32, stride=16), :] for p in range(4)]
        rows = [choose(blocks, i) for i in range(4)]
        halves.append(jnp.concatenate([pltpu.roll(x, LANES - 32 * i, 1) if i else x for i, x in enumerate(rows)], axis=0))
    return jnp.concatenate(halves, axis=1)


def pack_kernel(
    index_ref,
    previous_ref,
    current_ref,
    energies_ref,
    conduction_ref,
    valence_ref,
    kernel_ref,
    pick_ref,
    packed_ref,
    high_ref,
    low_ref,
    weights_ref,
    given,
    mine,
    momenta,
    picked,
    turned,
    arrived,
    fixed,
):
    fields = [
        pltpu.make_async_copy(ref, to, arrived.at[i])
        for i, (ref, to) in enumerate(
            (
                (current_ref, packed_ref.at[:, 0]),
                (energies_ref, given.at[0]),
                (previous_ref, given.at[1]),
                (conduction_ref, packed_ref.at[:, 1]),
            )
        )
    ]
    copies = [
        pltpu.make_async_copy(ref, to, fixed.at[i])
        for i, (ref, to) in enumerate(
            ((valence_ref.at[index_ref[0]], mine), (kernel_ref, momenta), (pick_ref, picked))
        )
    ]
    for copy in copies + fields:
        copy.start()
    copies[0].wait()
    flipped = mine[...].T
    for half in range(2):
        columns = slice(half * LANES, (half + 1) * LANES)
        turned[half] = flipped[:, columns]
        for row in range(8):
            high, low = split(turned[half, pl.ds(row, 32, stride=8), :])
            high_ref[row * 32 : row * 32 + 32, columns] = high
            low_ref[row * 32 : row * 32 + 32, columns] = low
    copies[1].wait()
    copies[2].wait()
    turn = index_ref[0] % 4
    starts = [pl.multiple_of((4 * part + (g + 4 - turn) % 4) * 32, 32) for part in range(2) for g in range(4)]
    rest = jnp.concatenate([momenta[pl.ds(start, 32), :] for start in starts], axis=0)
    total = rest.shape[0]
    weights = jnp.zeros((total, total), F32)
    for _ in range(3):
        part = rest.astype(BF16)
        rest = rest - part.astype(F32)
        weights += lax.dot_general(picked[...], part, NT, preferred_element_type=F32)
    weights_ref[...] = weights * (1.0 / total)
    for copy in fields:
        copy.wait()
    packed_ref[:, 2] = 2.0 * given[0] * packed_ref[:, 0] - given[1]


def square(ref, which):
    block = ref[:, which]
    return block.reshape(block.shape[0] * block.shape[1], block.shape[2])


def first_pairs_kernel(whole_ref, high_ref, low_ref, out_ref, turned_high_ref, turned_low_ref):
    conduct = split(square(whole_ref, 1))
    field = split(square(whole_ref, 0))
    inner = [split(dot3((conduct[0][rows], conduct[1][rows]), field)) for rows in (slice(0, LANES), slice(LANES, None))]
    inner = [jnp.concatenate([inner[0][i], inner[1][i]], axis=0) for i in range(2)]
    turned_high_ref[...], turned_low_ref[...] = split(square(whole_ref, 1).T)
    store_messages(dot3((high_ref[...], low_ref[...]), inner, NT), out_ref)


def screen_kernel(owned_ref, rows_high, rows_low, back_high, back_low, weights_ref, out_ref):
    total = weights_ref.shape[0]
    owned = split(jnp.concatenate([owned_ref[pl.ds(part, total, stride=2), :] for part in range(2)], axis=1))
    modes = []
    for part in range(2):
        mine = slice(part * LANES, (part + 1) * LANES)
        modes.append(split(dot3((rows_high[mine], rows_low[mine]), owned) * weights_ref[mine]))
    modes = [jnp.concatenate([modes[0][i], modes[1][i]], axis=0) for i in range(2)]
    for piece in range(2):
        mine = slice(piece * LANES, (piece + 1) * LANES)
        screened = dot3((back_high[mine], back_low[mine]), modes)
        for part in range(2):
            lines = pl.ds(2 * piece * LANES + part, LANES, stride=2)
            out_ref[lines, :] = screened[:, part * LANES : (part + 1) * LANES]


def product_back(screened_ref, turned, valence):
    screened = jnp.concatenate([load_messages(screened_ref, part) for part in range(2)], axis=0)
    return dot3(split(dot3(turned, split(screened), NT)), valence)


def next_pairs_kernel(screened_ref, whole_ref, high_ref, low_ref, turned_high_ref, turned_low_ref, next_ref, out_ref):
    conduct = split(square(whole_ref, 1))
    turned = turned_high_ref[...], turned_low_ref[...]
    valence = high_ref[...], low_ref[...]
    following = square(whole_ref, 2) + 2.0 * product_back(screened_ref, turned, valence)
    next_ref[...] = following
    field = split(following)
    inner = [split(dot3((conduct[0][rows], conduct[1][rows]), field)) for rows in (slice(0, LANES), slice(LANES, None))]
    inner = [jnp.concatenate([inner[0][i], inner[1][i]], axis=0) for i in range(2)]
    store_messages(dot3(valence, inner, NT), out_ref)


def last_kernel(screened_ref, whole_ref, high_ref, low_ref, next_ref, out_ref):
    conduct = split(square(whole_ref, 1))
    second = 0.0
    for part in range(2):
        mine = slice(part * LANES, (part + 1) * LANES)
        partial = dot3(split(load_messages(screened_ref, part)), conduct)
        second += dot3(split(partial.T), (high_ref[mine, :], low_ref[mine, :]))
    shape = out_ref.shape[0], out_ref.shape[2], out_ref.shape[3]
    out_ref[:, 0] = next_ref[...].reshape(shape)
    out_ref[:, 1] = second.reshape(shape)


def call(kernel, outs, flops, moved, **more):
    return pl.pallas_call(
        kernel,
        out_shape=outs,
        compiler_params=pltpu.CompilerParams(vmem_limit_bytes=VMEM_BYTES),
        cost_estimate=pl.CostEstimate(flops=flops, bytes_accessed=moved, transcendentals=0),
        **more,
    )


def on_device(previous, current, energies, valence, conduction, kernel):
    total = kernel.shape[0]
    rows, pick = real_transform(total)
    both = ("ka", "pa")
    banded = lambda x: jnp.swapaxes(x, 1, 2)
    per_k, bands, slim = current.shape
    flops = 2 * total**3
    size = 4 * total**2
    shaped = jax.ShapeDtypeStruct
    tables = [jnp.asarray(t) for t in (*split_table(rows), *split_table(rows.T.copy()))]

    far = pl.BlockSpec(memory_space=pltpu.HBM)
    near = pl.BlockSpec(memory_space=pltpu.VMEM)
    packed, high, low, weights = pl.pallas_call(
        pack_kernel,
        out_shape=[shaped((per_k, 3, slim, bands), F32)]
        + [shaped((total, bands), BF16)] * 2
        + [shaped((total, total), F32)],
        in_specs=[pl.BlockSpec(memory_space=pltpu.SMEM)] + [far] * 7,
        out_specs=[near] * 4,
        scratch_shapes=[
            pltpu.VMEM((2, per_k, slim, bands), F32),
            pltpu.VMEM((bands, total), F32),
            pltpu.VMEM((total, total), F32),
            pltpu.VMEM((total, total), BF16),
            pltpu.VMEM((2, total, LANES), F32),
            pltpu.SemaphoreType.DMA((4,)),
            pltpu.SemaphoreType.DMA((3,)),
        ],
        compiler_params=pltpu.CompilerParams(vmem_limit_bytes=VMEM_BYTES),
        cost_estimate=pl.CostEstimate(flops=3 * flops, bytes_accessed=12 * size, transcendentals=0),
    )(
        lax.axis_index("pa").reshape(1),
        *(
            pltpu.with_memory_space_constraint(x, pltpu.HBM)
            for x in (
                banded(previous),
                banded(current),
                banded(energies),
                banded(conduction),
                valence,
                jnp.transpose(kernel, (1, 2, 0)).reshape(total, total),
                jnp.asarray(pick.astype(BF16)),
            )
        ),
    )
    whole = lax.all_to_all(packed, "pa", split_axis=0, concat_axis=0, tiled=True)

    def exchange(block):
        block = block.reshape(total, 2, LANES)
        block = lax.all_to_all(block, both, split_axis=0, concat_axis=0, tiled=True)
        return block.reshape(2 * total, LANES)

    message = shaped((2 * total, LANES), F32)
    screen = call(screen_kernel, message, 6 * flops, 5 * size)

    part = shaped((total, total), BF16)
    pairs, *turned = call(first_pairs_kernel, [message, part, part], 6 * flops, 5 * size)(whole, high, low)
    back = exchange(screen(exchange(pairs), *tables, weights))
    following, pairs = call(next_pairs_kernel, [shaped((total, bands), F32), message], 12 * flops, 6 * size)(
        back, whole, high, low, *turned
    )
    back = exchange(screen(exchange(pairs), *tables, weights))
    home = call(last_kernel, shaped((per_k, 2, slim, bands), F32), 6 * flops, 6 * size)(
        back, whole, high, low, following
    )
    home = lax.all_to_all(home, "pa", split_axis=0, concat_axis=0, tiled=True)
    next_one = banded(home[:, 0])
    next_two = 2.0 * (energies * next_one + banded(home[:, 1])) - current
    return next_one, next_two


def solution(mesh):
    banded = P("ka", None, "pa")
    return jax.shard_map(
        on_device,
        mesh=mesh,
        in_specs=(banded, banded, banded, P("ka", None, None), banded, P(None, "ka", "pa")),
        out_specs=(banded, banded),
        check_vma=False,
    )
```

```python
import math

import jax
import jax.numpy as jnp
import numpy as np
from jax import lax
from jax.experimental import pallas as pl
from jax.experimental.pallas import tpu as pltpu
from jax.sharding import PartitionSpec as P

KY = 16
LANES = 128
VMEM_BYTES = 16 * 1024 * 1024
F32 = jnp.float32
BF16 = jnp.bfloat16
NN = (((1,), (0,)), ((), ()))
NT = (((1,), (1,)), ((), ()))


def real_transform(total):
    wide = total // KY
    points = np.arange(total)
    coarse, finer = points // KY, points % KY
    mirror = (-coarse % wide) * KY + (-finer % KY)
    turns = (coarse[:, None] * coarse[None, :] % wide) / wide
    turns = turns + (finer[:, None] * finer[None, :] % KY) / KY
    angles = 2.0 * math.pi * turns
    rows = np.where((points <= mirror)[:, None], np.cos(angles), np.sin(angles))
    return rows.astype(np.float32)


def pair_sums(total):
    row = lax.broadcasted_iota(jnp.int32, (total, total), 0)
    column = lax.broadcasted_iota(jnp.int32, (total, total), 1)
    wide = total // KY
    bits = KY.bit_length() - 1
    mirror = (((wide - (row >> bits)) & (wide - 1)) << bits) + ((KY - (row & (KY - 1))) & (KY - 1))
    return jnp.where((column == row) | (column == mirror), 1.0, 0.0).astype(BF16)


def split_table(table):
    high = table.astype(BF16)
    return high, (table - high.astype(np.float32)).astype(BF16)


def split(x):
    high = x.astype(BF16)
    return high, (x - high.astype(F32)).astype(BF16)


def dot3(a, b, dims=NN):
    left = jnp.concatenate([a[0], a[0], a[1]], axis=1)
    right = jnp.concatenate([b[0], b[1], b[0]], axis=dims[0][1][0])
    return lax.dot_general(left, right, dims, preferred_element_type=F32)


def choose(blocks, which):
    group = lax.broadcasted_iota(jnp.int32, blocks[0].shape, 1) // 32
    chosen = [blocks[(g - which) % 4] for g in range(4)]
    low = jnp.where(group == 0, chosen[0], chosen[1])
    high = jnp.where(group == 2, chosen[2], chosen[3])
    return jnp.where(group < 2, low, high)


def store_messages(pairs, out_ref):
    for half in range(2):
        for part in range(2):
            blocks = []
            for i in range(4):
                start = (4 * part + i) * 32
                block = pairs[start : start + 32, half * LANES : (half + 1) * LANES]
                blocks.append(pltpu.roll(block, 32 * i, 1) if i else block)
            for p in range(4):
                out_ref[pl.ds((half * 4 + p) * 2 + part, 32, stride=16), :] = choose(blocks, p)


def load_messages(in_ref, part):
    halves = []
    for half in range(2):
        blocks = [in_ref[pl.ds((half * 4 + p) * 2 + part, 32, stride=16), :] for p in range(4)]
        rows = [choose(blocks, i) for i in range(4)]
        halves.append(jnp.concatenate([pltpu.roll(x, LANES - 32 * i, 1) if i else x for i, x in enumerate(rows)], axis=0))
    return jnp.concatenate(halves, axis=1)


def pack_kernel(
    index_ref,
    previous_ref,
    current_ref,
    energies_ref,
    conduction_ref,
    valence_ref,
    kernel_ref,
    packed_ref,
    high_ref,
    low_ref,
    weights_ref,
    given,
    mine,
    momenta,
    turned,
    arrived,
    fixed,
):
    fields = [
        pltpu.make_async_copy(ref, to, arrived.at[i])
        for i, (ref, to) in enumerate(
            (
                (current_ref, packed_ref.at[:, 0]),
                (energies_ref, given.at[0]),
                (previous_ref, given.at[1]),
                (conduction_ref, packed_ref.at[:, 1]),
            )
        )
    ]
    copies = [
        pltpu.make_async_copy(ref, to, fixed.at[i])
        for i, (ref, to) in enumerate(
            ((valence_ref.at[index_ref[0]], mine), (kernel_ref, momenta))
        )
    ]
    for copy in copies + fields:
        copy.start()
    copies[0].wait()
    flipped = mine[...].T
    for half in range(2):
        columns = slice(half * LANES, (half + 1) * LANES)
        turned[half] = flipped[:, columns]
        for row in range(8):
            high, low = split(turned[half, pl.ds(row, 32, stride=8), :])
            high_ref[row * 32 : row * 32 + 32, columns] = high
            low_ref[row * 32 : row * 32 + 32, columns] = low
    copies[1].wait()
    turn = index_ref[0] % 4
    starts = [pl.multiple_of((4 * part + (g + 4 - turn) % 4) * 32, 32) for part in range(2) for g in range(4)]
    rest = jnp.concatenate([momenta[pl.ds(start, 32), :] for start in starts], axis=0)
    total = rest.shape[0]
    weights = jnp.zeros((total, total), F32)
    picked = pair_sums(total)
    for part in split(rest):
        weights += lax.dot_general(picked, part, NT, preferred_element_type=F32)
    weights_ref[...] = weights * (1.0 / total)
    for copy in fields:
        copy.wait()
    packed_ref[:, 2] = 2.0 * given[0] * packed_ref[:, 0] - given[1]


def square(ref, which):
    block = ref[:, which]
    return block.reshape(block.shape[0] * block.shape[1], block.shape[2])


def first_pairs_kernel(whole_ref, high_ref, low_ref, out_ref, turned_high_ref, turned_low_ref):
    conduct = split(square(whole_ref, 1))
    field = split(square(whole_ref, 0))
    inner = [split(dot3((conduct[0][rows], conduct[1][rows]), field)) for rows in (slice(0, LANES), slice(LANES, None))]
    inner = [jnp.concatenate([inner[0][i], inner[1][i]], axis=0) for i in range(2)]
    turned_high_ref[...], turned_low_ref[...] = split(square(whole_ref, 1).T)
    store_messages(dot3((high_ref[...], low_ref[...]), inner, NT), out_ref)


def screen_kernel(owned_ref, rows_high, rows_low, back_high, back_low, weights_ref, out_ref):
    total = weights_ref.shape[0]
    owned = split(jnp.concatenate([owned_ref[pl.ds(part, total, stride=2), :] for part in range(2)], axis=1))
    modes = []
    for part in range(2):
        mine = slice(part * LANES, (part + 1) * LANES)
        modes.append(split(dot3((rows_high[mine], rows_low[mine]), owned) * weights_ref[mine]))
    modes = [jnp.concatenate([modes[0][i], modes[1][i]], axis=0) for i in range(2)]
    for piece in range(2):
        mine = slice(piece * LANES, (piece + 1) * LANES)
        screened = dot3((back_high[mine], back_low[mine]), modes)
        for part in range(2):
            lines = pl.ds(2 * piece * LANES + part, LANES, stride=2)
            out_ref[lines, :] = screened[:, part * LANES : (part + 1) * LANES]


def product_back(screened_ref, turned, valence):
    screened = jnp.concatenate([load_messages(screened_ref, part) for part in range(2)], axis=0)
    return dot3(split(dot3(turned, split(screened), NT)), valence)


def next_pairs_kernel(screened_ref, whole_ref, high_ref, low_ref, turned_high_ref, turned_low_ref, next_ref, out_ref):
    conduct = split(square(whole_ref, 1))
    turned = turned_high_ref[...], turned_low_ref[...]
    valence = high_ref[...], low_ref[...]
    following = square(whole_ref, 2) + 2.0 * product_back(screened_ref, turned, valence)
    next_ref[...] = following
    field = split(following)
    inner = [split(dot3((conduct[0][rows], conduct[1][rows]), field)) for rows in (slice(0, LANES), slice(LANES, None))]
    inner = [jnp.concatenate([inner[0][i], inner[1][i]], axis=0) for i in range(2)]
    store_messages(dot3(valence, inner, NT), out_ref)


def last_kernel(screened_ref, whole_ref, high_ref, low_ref, next_ref, out_ref):
    conduct = split(square(whole_ref, 1))
    second = 0.0
    for part in range(2):
        mine = slice(part * LANES, (part + 1) * LANES)
        partial = dot3(split(load_messages(screened_ref, part)), conduct)
        second += dot3(split(partial.T), (high_ref[mine, :], low_ref[mine, :]))
    shape = out_ref.shape[0], out_ref.shape[2], out_ref.shape[3]
    out_ref[:, 0] = next_ref[...].reshape(shape)
    out_ref[:, 1] = second.reshape(shape)


def call(kernel, outs, flops, moved, **more):
    return pl.pallas_call(
        kernel,
        out_shape=outs,
        compiler_params=pltpu.CompilerParams(vmem_limit_bytes=VMEM_BYTES),
        cost_estimate=pl.CostEstimate(flops=flops, bytes_accessed=moved, transcendentals=0),
        **more,
    )


def on_device(previous, current, energies, valence, conduction, kernel):
    total = kernel.shape[0]
    rows = real_transform(total)
    both = ("ka", "pa")
    banded = lambda x: jnp.swapaxes(x, 1, 2)
    per_k, bands, slim = current.shape
    flops = 2 * total**3
    size = 4 * total**2
    shaped = jax.ShapeDtypeStruct
    tables = [jnp.asarray(t) for t in (*split_table(rows), *split_table(rows.T.copy()))]

    far = pl.BlockSpec(memory_space=pltpu.HBM)
    near = pl.BlockSpec(memory_space=pltpu.VMEM)
    packed, high, low, weights = pl.pallas_call(
        pack_kernel,
        out_shape=[shaped((per_k, 3, slim, bands), F32)]
        + [shaped((total, bands), BF16)] * 2
        + [shaped((total, total), F32)],
        in_specs=[pl.BlockSpec(memory_space=pltpu.SMEM)] + [far] * 6,
        out_specs=[near] * 4,
        scratch_shapes=[
            pltpu.VMEM((2, per_k, slim, bands), F32),
            pltpu.VMEM((bands, total), F32),
            pltpu.VMEM((total, total), F32),
            pltpu.VMEM((2, total, LANES), F32),
            pltpu.SemaphoreType.DMA((4,)),
            pltpu.SemaphoreType.DMA((2,)),
        ],
        compiler_params=pltpu.CompilerParams(vmem_limit_bytes=VMEM_BYTES),
        cost_estimate=pl.CostEstimate(flops=3 * flops, bytes_accessed=12 * size, transcendentals=0),
    )(
        lax.axis_index("pa").reshape(1),
        *(
            pltpu.with_memory_space_constraint(x, pltpu.HBM)
            for x in (
                banded(previous),
                banded(current),
                banded(energies),
                banded(conduction),
                valence,
                jnp.transpose(kernel, (1, 2, 0)).reshape(total, total),
            )
        ),
    )
    whole = lax.all_to_all(packed, "pa", split_axis=0, concat_axis=0, tiled=True)

    def exchange(block):
        block = block.reshape(total, 2, LANES)
        block = lax.all_to_all(block, both, split_axis=0, concat_axis=0, tiled=True)
        return block.reshape(2 * total, LANES)

    message = shaped((2 * total, LANES), F32)
    screen = call(screen_kernel, message, 6 * flops, 5 * size)

    part = shaped((total, total), BF16)
    pairs, *turned = call(first_pairs_kernel, [message, part, part], 6 * flops, 5 * size)(whole, high, low)
    back = exchange(screen(exchange(pairs), *tables, weights))
    following, pairs = call(next_pairs_kernel, [shaped((total, bands), F32), message], 12 * flops, 6 * size)(
        back, whole, high, low, *turned
    )
    back = exchange(screen(exchange(pairs), *tables, weights))
    home = call(last_kernel, shaped((per_k, 2, slim, bands), F32), 6 * flops, 6 * size)(
        back, whole, high, low, following
    )
    home = lax.all_to_all(home, "pa", split_axis=0, concat_axis=0, tiled=True)
    next_one = banded(home[:, 0])
    next_two = 2.0 * (energies * next_one + banded(home[:, 1])) - current
    return next_one, next_two


def solution(mesh):
    banded = P("ka", None, "pa")
    return jax.shard_map(
        on_device,
        mesh=mesh,
        in_specs=(banded, banded, banded, P("ka", None, None), banded, P(None, "ka", "pa")),
        out_specs=(banded, banded),
        check_vma=False,
    )
```

```python
import math

import jax
import jax.numpy as jnp
import numpy as np
from jax import lax
from jax.experimental import pallas as pl
from jax.experimental.pallas import tpu as pltpu
from jax.sharding import PartitionSpec as P

KY = 16
LANES = 128
VMEM_BYTES = 16 * 1024 * 1024
F32 = jnp.float32
BF16 = jnp.bfloat16
NN = (((1,), (0,)), ((), ()))
NT = (((1,), (1,)), ((), ()))


def real_transform(total):
    wide = total // KY
    points = np.arange(total)
    coarse, finer = points // KY, points % KY
    mirror = (-coarse % wide) * KY + (-finer % KY)
    turns = (coarse[:, None] * coarse[None, :] % wide) / wide
    turns = turns + (finer[:, None] * finer[None, :] % KY) / KY
    angles = 2.0 * math.pi * turns
    rows = np.where((points <= mirror)[:, None], np.cos(angles), np.sin(angles))
    return rows.astype(np.float32)


def pair_sums(total):
    row = lax.broadcasted_iota(jnp.int32, (total, total), 0)
    column = lax.broadcasted_iota(jnp.int32, (total, total), 1)
    wide = total // KY
    bits = KY.bit_length() - 1
    mirror = (((wide - (row >> bits)) & (wide - 1)) << bits) + ((KY - (row & (KY - 1))) & (KY - 1))
    return jnp.where((column == row) | (column == mirror), 1.0, 0.0).astype(BF16)


def split_table(table):
    high = table.astype(BF16)
    return high, (table - high.astype(np.float32)).astype(BF16)


def split(x):
    high = x.astype(BF16)
    return high, (x - high.astype(F32)).astype(BF16)


def dot3(a, b, dims=NN):
    left = jnp.concatenate([a[0], a[0], a[1]], axis=1)
    right = jnp.concatenate([b[0], b[1], b[0]], axis=dims[0][1][0])
    return lax.dot_general(left, right, dims, preferred_element_type=F32)


def choose(blocks, which):
    group = lax.broadcasted_iota(jnp.int32, blocks[0].shape, 1) // 32
    chosen = [blocks[(g - which) % 4] for g in range(4)]
    low = jnp.where(group == 0, chosen[0], chosen[1])
    high = jnp.where(group == 2, chosen[2], chosen[3])
    return jnp.where(group < 2, low, high)


def store_messages(pairs, out_ref):
    for half in range(2):
        for part in range(2):
            blocks = []
            for i in range(4):
                start = (4 * part + i) * 32
                block = pairs[start : start + 32, half * LANES : (half + 1) * LANES]
                blocks.append(pltpu.roll(block, 32 * i, 1) if i else block)
            for p in range(4):
                out_ref[pl.ds((half * 4 + p) * 2 + part, 32, stride=16), :] = choose(blocks, p)


def load_messages(in_ref, part):
    halves = []
    for half in range(2):
        blocks = [in_ref[pl.ds((half * 4 + p) * 2 + part, 32, stride=16), :] for p in range(4)]
        rows = [choose(blocks, i) for i in range(4)]
        halves.append(jnp.concatenate([pltpu.roll(x, LANES - 32 * i, 1) if i else x for i, x in enumerate(rows)], axis=0))
    return jnp.concatenate(halves, axis=1)


def pack_kernel(
    index_ref,
    previous_ref,
    current_ref,
    energies_ref,
    conduction_ref,
    valence_ref,
    kernel_ref,
    packed_ref,
    high_ref,
    low_ref,
    weights_ref,
    given,
    mine,
    momenta,
    turned,
    arrived,
    fixed,
):
    fields = [
        pltpu.make_async_copy(ref, to, arrived.at[i])
        for i, (ref, to) in enumerate(
            (
                (current_ref, packed_ref.at[:, 0]),
                (energies_ref, given.at[0]),
                (previous_ref, given.at[1]),
                (conduction_ref, packed_ref.at[:, 1]),
            )
        )
    ]
    copies = [
        pltpu.make_async_copy(ref, to, fixed.at[i])
        for i, (ref, to) in enumerate(
            ((valence_ref.at[index_ref[0]], mine), (kernel_ref, momenta))
        )
    ]
    for copy in copies + fields:
        copy.start()
    copies[0].wait()
    flipped = mine[...].T
    for half in range(2):
        columns = slice(half * LANES, (half + 1) * LANES)
        turned[half] = flipped[:, columns]
        for row in range(8):
            high, low = split(turned[half, pl.ds(row, 32, stride=8), :])
            high_ref[row * 32 : row * 32 + 32, columns] = high
            low_ref[row * 32 : row * 32 + 32, columns] = low
    copies[1].wait()
    turn = index_ref[0] % 4
    starts = [pl.multiple_of((4 * part + (g + 4 - turn) % 4) * 32, 32) for part in range(2) for g in range(4)]
    rest = jnp.concatenate([momenta[pl.ds(start, 32), :] for start in starts], axis=0)
    total = rest.shape[0]
    weights = jnp.zeros((total, total), F32)
    picked = pair_sums(total)
    for part in split(rest):
        weights += lax.dot_general(picked, part, NT, preferred_element_type=F32)
    weights_ref[...] = weights * (1.0 / total)
    for copy in fields:
        copy.wait()
    packed_ref[:, 2] = 2.0 * given[0] * packed_ref[:, 0] - given[1]


def square(ref, which):
    block = ref[:, which]
    return block.reshape(block.shape[0] * block.shape[1], block.shape[2])


def first_pairs_kernel(whole_ref, high_ref, low_ref, out_ref, turned_high_ref, turned_low_ref, conduct_high_ref, conduct_low_ref):
    conduct = split(square(whole_ref, 1))
    conduct_high_ref[...], conduct_low_ref[...] = conduct
    field = split(square(whole_ref, 0))
    inner = [split(dot3((conduct[0][rows], conduct[1][rows]), field)) for rows in (slice(0, LANES), slice(LANES, None))]
    inner = [jnp.concatenate([inner[0][i], inner[1][i]], axis=0) for i in range(2)]
    turned_high_ref[...], turned_low_ref[...] = split(square(whole_ref, 1).T)
    store_messages(dot3((high_ref[...], low_ref[...]), inner, NT), out_ref)


def screen_kernel(owned_ref, rows_high, rows_low, back_high, back_low, weights_ref, out_ref):
    total = weights_ref.shape[0]
    owned = split(jnp.concatenate([owned_ref[pl.ds(part, total, stride=2), :] for part in range(2)], axis=1))
    modes = []
    for part in range(2):
        mine = slice(part * LANES, (part + 1) * LANES)
        modes.append(split(dot3((rows_high[mine], rows_low[mine]), owned) * weights_ref[mine]))
    modes = [jnp.concatenate([modes[0][i], modes[1][i]], axis=0) for i in range(2)]
    for piece in range(2):
        mine = slice(piece * LANES, (piece + 1) * LANES)
        screened = dot3((back_high[mine], back_low[mine]), modes)
        for part in range(2):
            lines = pl.ds(2 * piece * LANES + part, LANES, stride=2)
            out_ref[lines, :] = screened[:, part * LANES : (part + 1) * LANES]


def product_back(screened_ref, turned, valence):
    screened = jnp.concatenate([load_messages(screened_ref, part) for part in range(2)], axis=0)
    return dot3(split(dot3(turned, split(screened), NT)), valence)


def next_pairs_kernel(screened_ref, whole_ref, high_ref, low_ref, turned_high_ref, turned_low_ref, conduct_high_ref, conduct_low_ref, next_ref, out_ref):
    conduct = conduct_high_ref[...], conduct_low_ref[...]
    turned = turned_high_ref[...], turned_low_ref[...]
    valence = high_ref[...], low_ref[...]
    following = square(whole_ref, 2) + 2.0 * product_back(screened_ref, turned, valence)
    next_ref[...] = following
    field = split(following)
    inner = [split(dot3((conduct[0][rows], conduct[1][rows]), field)) for rows in (slice(0, LANES), slice(LANES, None))]
    inner = [jnp.concatenate([inner[0][i], inner[1][i]], axis=0) for i in range(2)]
    store_messages(dot3(valence, inner, NT), out_ref)


def last_kernel(screened_ref, high_ref, low_ref, conduct_high_ref, conduct_low_ref, next_ref, out_ref):
    conduct = conduct_high_ref[...], conduct_low_ref[...]
    second = 0.0
    for part in range(2):
        mine = slice(part * LANES, (part + 1) * LANES)
        partial = dot3(split(load_messages(screened_ref, part)), conduct)
        second += dot3(split(partial.T), (high_ref[mine, :], low_ref[mine, :]))
    shape = out_ref.shape[0], out_ref.shape[2], out_ref.shape[3]
    out_ref[:, 0] = next_ref[...].reshape(shape)
    out_ref[:, 1] = second.reshape(shape)


def call(kernel, outs, flops, moved, **more):
    return pl.pallas_call(
        kernel,
        out_shape=outs,
        compiler_params=pltpu.CompilerParams(vmem_limit_bytes=VMEM_BYTES),
        cost_estimate=pl.CostEstimate(flops=flops, bytes_accessed=moved, transcendentals=0),
        **more,
    )


def on_device(previous, current, energies, valence, conduction, kernel):
    total = kernel.shape[0]
    rows = real_transform(total)
    both = ("ka", "pa")
    banded = lambda x: jnp.swapaxes(x, 1, 2)
    per_k, bands, slim = current.shape
    flops = 2 * total**3
    size = 4 * total**2
    shaped = jax.ShapeDtypeStruct
    tables = [jnp.asarray(t) for t in (*split_table(rows), *split_table(rows.T.copy()))]

    far = pl.BlockSpec(memory_space=pltpu.HBM)
    near = pl.BlockSpec(memory_space=pltpu.VMEM)
    packed, high, low, weights = pl.pallas_call(
        pack_kernel,
        out_shape=[shaped((per_k, 3, slim, bands), F32)]
        + [shaped((total, bands), BF16)] * 2
        + [shaped((total, total), F32)],
        in_specs=[pl.BlockSpec(memory_space=pltpu.SMEM)] + [far] * 6,
        out_specs=[near] * 4,
        scratch_shapes=[
            pltpu.VMEM((2, per_k, slim, bands), F32),
            pltpu.VMEM((bands, total), F32),
            pltpu.VMEM((total, total), F32),
            pltpu.VMEM((2, total, LANES), F32),
            pltpu.SemaphoreType.DMA((4,)),
            pltpu.SemaphoreType.DMA((2,)),
        ],
        compiler_params=pltpu.CompilerParams(vmem_limit_bytes=VMEM_BYTES),
        cost_estimate=pl.CostEstimate(flops=3 * flops, bytes_accessed=12 * size, transcendentals=0),
    )(
        lax.axis_index("pa").reshape(1),
        *(
            pltpu.with_memory_space_constraint(x, pltpu.HBM)
            for x in (
                banded(previous),
                banded(current),
                banded(energies),
                banded(conduction),
                valence,
                jnp.transpose(kernel, (1, 2, 0)).reshape(total, total),
            )
        ),
    )
    whole = lax.all_to_all(packed, "pa", split_axis=0, concat_axis=0, tiled=True)

    def exchange(block):
        block = block.reshape(total, 2, LANES)
        block = lax.all_to_all(block, both, split_axis=0, concat_axis=0, tiled=True)
        return block.reshape(2 * total, LANES)

    message = shaped((2 * total, LANES), F32)
    screen = call(screen_kernel, message, 6 * flops, 5 * size)

    part = shaped((total, total), BF16)
    pairs, *parts = call(first_pairs_kernel, [message] + [part] * 4, 6 * flops, 5 * size)(whole, high, low)
    back = exchange(screen(exchange(pairs), *tables, weights))
    following, pairs = call(next_pairs_kernel, [shaped((total, bands), F32), message], 12 * flops, 6 * size)(
        back, whole, high, low, *parts
    )
    back = exchange(screen(exchange(pairs), *tables, weights))
    home = call(last_kernel, shaped((per_k, 2, slim, bands), F32), 6 * flops, 6 * size)(
        back, high, low, *parts[2:], following
    )
    home = lax.all_to_all(home, "pa", split_axis=0, concat_axis=0, tiled=True)
    next_one = banded(home[:, 0])
    next_two = 2.0 * (energies * next_one + banded(home[:, 1])) - current
    return next_one, next_two


def solution(mesh):
    banded = P("ka", None, "pa")
    return jax.shard_map(
        on_device,
        mesh=mesh,
        in_specs=(banded, banded, banded, P("ka", None, None), banded, P(None, "ka", "pa")),
        out_specs=(banded, banded),
        check_vma=False,
    )
```

```python
import math

import jax
import jax.numpy as jnp
import numpy as np
from jax import lax
from jax.experimental import pallas as pl
from jax.experimental.pallas import tpu as pltpu
from jax.sharding import PartitionSpec as P

KY = 16
LANES = 128
VMEM_BYTES = 16 * 1024 * 1024
F32 = jnp.float32
BF16 = jnp.bfloat16
NN = (((1,), (0,)), ((), ()))
NT = (((1,), (1,)), ((), ()))


def real_transform(total):
    wide = total // KY
    points = np.arange(total)
    coarse, finer = points // KY, points % KY
    mirror = (-coarse % wide) * KY + (-finer % KY)
    turns = (coarse[:, None] * coarse[None, :] % wide) / wide
    turns = turns + (finer[:, None] * finer[None, :] % KY) / KY
    angles = 2.0 * math.pi * turns
    rows = np.where((points <= mirror)[:, None], np.cos(angles), np.sin(angles))
    return rows.astype(np.float32)


def pair_sums(total):
    row = lax.broadcasted_iota(jnp.int32, (total, total), 0)
    column = lax.broadcasted_iota(jnp.int32, (total, total), 1)
    wide = total // KY
    bits = KY.bit_length() - 1
    mirror = (((wide - (row >> bits)) & (wide - 1)) << bits) + ((KY - (row & (KY - 1))) & (KY - 1))
    return jnp.where((column == row) | (column == mirror), 1.0, 0.0).astype(BF16)


def split_table(table):
    high = table.astype(BF16)
    return high, (table - high.astype(np.float32)).astype(BF16)


def split(x):
    high = x.astype(BF16)
    return high, (x - high.astype(F32)).astype(BF16)


def dot3(a, b, dims=NN):
    left = jnp.concatenate([a[0], a[0], a[1]], axis=1)
    right = jnp.concatenate([b[0], b[1], b[0]], axis=dims[0][1][0])
    return lax.dot_general(left, right, dims, preferred_element_type=F32)


def choose(blocks, which):
    group = lax.broadcasted_iota(jnp.int32, blocks[0].shape, 1) // 32
    chosen = [blocks[(g - which) % 4] for g in range(4)]
    low = jnp.where(group == 0, chosen[0], chosen[1])
    high = jnp.where(group == 2, chosen[2], chosen[3])
    return jnp.where(group < 2, low, high)


def store_messages(pairs, out_ref):
    for half in range(2):
        for part in range(2):
            blocks = []
            for i in range(4):
                start = (4 * part + i) * 32
                block = pairs[start : start + 32, half * LANES : (half + 1) * LANES]
                blocks.append(pltpu.roll(block, 32 * i, 1) if i else block)
            for p in range(4):
                out_ref[pl.ds((half * 4 + p) * 2 + part, 32, stride=16), :] = choose(blocks, p)


def load_messages(in_ref, part):
    halves = []
    for half in range(2):
        blocks = [in_ref[pl.ds((half * 4 + p) * 2 + part, 32, stride=16), :] for p in range(4)]
        rows = [choose(blocks, i) for i in range(4)]
        halves.append(jnp.concatenate([pltpu.roll(x, LANES - 32 * i, 1) if i else x for i, x in enumerate(rows)], axis=0))
    return jnp.concatenate(halves, axis=1)


def pack_kernel(
    index_ref,
    previous_ref,
    current_ref,
    energies_ref,
    conduction_ref,
    valence_ref,
    kernel_ref,
    packed_ref,
    high_ref,
    low_ref,
    weights_ref,
    given,
    mine,
    momenta,
    turned,
    arrived,
    fixed,
):
    fields = [
        pltpu.make_async_copy(ref, to, arrived.at[i])
        for i, (ref, to) in enumerate(
            (
                (current_ref, packed_ref.at[:, 0]),
                (energies_ref, given.at[0]),
                (previous_ref, given.at[1]),
                (conduction_ref, packed_ref.at[:, 1]),
            )
        )
    ]
    copies = [
        pltpu.make_async_copy(ref, to, fixed.at[i])
        for i, (ref, to) in enumerate(
            ((valence_ref.at[index_ref[0]], mine), (kernel_ref, momenta))
        )
    ]
    for copy in copies + fields:
        copy.start()
    copies[0].wait()
    flipped = mine[...].T
    for half in range(2):
        columns = slice(half * LANES, (half + 1) * LANES)
        turned[half] = flipped[:, columns]
        for row in range(8):
            high, low = split(turned[half, pl.ds(row, 32, stride=8), :])
            high_ref[row * 32 : row * 32 + 32, columns] = high
            low_ref[row * 32 : row * 32 + 32, columns] = low
    copies[1].wait()
    turn = index_ref[0] % 4
    starts = [pl.multiple_of((4 * part + (g + 4 - turn) % 4) * 32, 32) for part in range(2) for g in range(4)]
    rest = jnp.concatenate([momenta[pl.ds(start, 32), :] for start in starts], axis=0)
    total = rest.shape[0]
    weights = jnp.zeros((total, total), F32)
    picked = pair_sums(total)
    for part in split(rest):
        weights += lax.dot_general(picked, part, NT, preferred_element_type=F32)
    weights_ref[...] = weights * (1.0 / total)
    for copy in fields:
        copy.wait()
    packed_ref[:, 2] = 2.0 * given[0] * packed_ref[:, 0] - given[1]


def square(ref, which):
    block = ref[:, which]
    return block.reshape(block.shape[0] * block.shape[1], block.shape[2])


def first_pairs_kernel(whole_ref, high_ref, low_ref, out_ref, turned_high_ref, turned_low_ref, conduct_high_ref, conduct_low_ref):
    conduct = split(square(whole_ref, 1))
    conduct_high_ref[...], conduct_low_ref[...] = conduct
    field = split(square(whole_ref, 0))
    inner = [split(dot3((conduct[0][rows], conduct[1][rows]), field)) for rows in (slice(0, LANES), slice(LANES, None))]
    inner = [jnp.concatenate([inner[0][i], inner[1][i]], axis=0) for i in range(2)]
    turned_high_ref[...], turned_low_ref[...] = split(square(whole_ref, 1).T)
    store_messages(dot3((high_ref[...], low_ref[...]), inner, NT), out_ref)


def screen_kernel(owned_ref, rows_high, rows_low, back_high, back_low, weights_ref, out_ref):
    total = weights_ref.shape[0]
    owned = split(jnp.concatenate([owned_ref[pl.ds(part, total, stride=2), :] for part in range(2)], axis=1))
    modes = []
    for part in range(2):
        mine = slice(part * LANES, (part + 1) * LANES)
        modes.append(split(dot3((rows_high[mine], rows_low[mine]), owned) * weights_ref[mine]))
    modes = [jnp.concatenate([modes[0][i], modes[1][i]], axis=0) for i in range(2)]
    for piece in range(2):
        mine = slice(piece * LANES, (piece + 1) * LANES)
        screened = dot3((back_high[mine], back_low[mine]), modes)
        for part in range(2):
            lines = pl.ds(2 * piece * LANES + part, LANES, stride=2)
            out_ref[lines, :] = screened[:, part * LANES : (part + 1) * LANES]


def product_back(screened_ref, turned, valence):
    screened = jnp.concatenate([load_messages(screened_ref, part) for part in range(2)], axis=0)
    return dot3(split(dot3(turned, split(screened), NT)), valence)


def next_pairs_kernel(screened_ref, whole_ref, high_ref, low_ref, turned_high_ref, turned_low_ref, conduct_high_ref, conduct_low_ref, next_ref, out_ref):
    conduct = conduct_high_ref[...], conduct_low_ref[...]
    turned = turned_high_ref[...], turned_low_ref[...]
    valence = high_ref[...], low_ref[...]
    following = square(whole_ref, 2) + 2.0 * product_back(screened_ref, turned, valence)
    next_ref[:, 0] = following.reshape(next_ref.shape[0], next_ref.shape[2], next_ref.shape[3])
    field = split(following)
    inner = [split(dot3((conduct[0][rows], conduct[1][rows]), field)) for rows in (slice(0, LANES), slice(LANES, None))]
    inner = [jnp.concatenate([inner[0][i], inner[1][i]], axis=0) for i in range(2)]
    store_messages(dot3(valence, inner, NT), out_ref)


def last_kernel(screened_ref, high_ref, low_ref, conduct_high_ref, conduct_low_ref, next_ref, out_ref):
    del next_ref
    conduct = conduct_high_ref[...], conduct_low_ref[...]
    second = 0.0
    for part in range(2):
        mine = slice(part * LANES, (part + 1) * LANES)
        partial = dot3(split(load_messages(screened_ref, part)), conduct)
        second += dot3(split(partial.T), (high_ref[mine, :], low_ref[mine, :]))
    shape = out_ref.shape[0], out_ref.shape[2], out_ref.shape[3]
    out_ref[:, 1] = second.reshape(shape)


def call(kernel, outs, flops, moved, **more):
    return pl.pallas_call(
        kernel,
        out_shape=outs,
        compiler_params=pltpu.CompilerParams(vmem_limit_bytes=VMEM_BYTES),
        cost_estimate=pl.CostEstimate(flops=flops, bytes_accessed=moved, transcendentals=0),
        **more,
    )


def on_device(previous, current, energies, valence, conduction, kernel):
    total = kernel.shape[0]
    rows = real_transform(total)
    both = ("ka", "pa")
    banded = lambda x: jnp.swapaxes(x, 1, 2)
    per_k, bands, slim = current.shape
    flops = 2 * total**3
    size = 4 * total**2
    shaped = jax.ShapeDtypeStruct
    tables = [jnp.asarray(t) for t in (*split_table(rows), *split_table(rows.T.copy()))]

    far = pl.BlockSpec(memory_space=pltpu.HBM)
    near = pl.BlockSpec(memory_space=pltpu.VMEM)
    packed, high, low, weights = pl.pallas_call(
        pack_kernel,
        out_shape=[shaped((per_k, 3, slim, bands), F32)]
        + [shaped((total, bands), BF16)] * 2
        + [shaped((total, total), F32)],
        in_specs=[pl.BlockSpec(memory_space=pltpu.SMEM)] + [far] * 6,
        out_specs=[near] * 4,
        scratch_shapes=[
            pltpu.VMEM((2, per_k, slim, bands), F32),
            pltpu.VMEM((bands, total), F32),
            pltpu.VMEM((total, total), F32),
            pltpu.VMEM((2, total, LANES), F32),
            pltpu.SemaphoreType.DMA((4,)),
            pltpu.SemaphoreType.DMA((2,)),
        ],
        compiler_params=pltpu.CompilerParams(vmem_limit_bytes=VMEM_BYTES),
        cost_estimate=pl.CostEstimate(flops=3 * flops, bytes_accessed=12 * size, transcendentals=0),
    )(
        lax.axis_index("pa").reshape(1),
        *(
            pltpu.with_memory_space_constraint(x, pltpu.HBM)
            for x in (
                banded(previous),
                banded(current),
                banded(energies),
                banded(conduction),
                valence,
                jnp.transpose(kernel, (1, 2, 0)).reshape(total, total),
            )
        ),
    )
    whole = lax.all_to_all(packed, "pa", split_axis=0, concat_axis=0, tiled=True)

    def exchange(block):
        block = block.reshape(total, 2, LANES)
        block = lax.all_to_all(block, both, split_axis=0, concat_axis=0, tiled=True)
        return block.reshape(2 * total, LANES)

    message = shaped((2 * total, LANES), F32)
    screen = call(screen_kernel, message, 6 * flops, 5 * size)

    part = shaped((total, total), BF16)
    pairs, *parts = call(first_pairs_kernel, [message] + [part] * 4, 6 * flops, 5 * size)(whole, high, low)
    back = exchange(screen(exchange(pairs), *tables, weights))
    following, pairs = call(next_pairs_kernel, [shaped((per_k, 2, slim, bands), F32), message], 12 * flops, 6 * size)(
        back, whole, high, low, *parts
    )
    back = exchange(screen(exchange(pairs), *tables, weights))
    home = call(last_kernel, shaped((per_k, 2, slim, bands), F32), 6 * flops, 6 * size, input_output_aliases={5: 0})(
        back, high, low, *parts[2:], following
    )
    home = lax.all_to_all(home, "pa", split_axis=0, concat_axis=0, tiled=True)
    next_one = banded(home[:, 0])
    next_two = 2.0 * (energies * next_one + banded(home[:, 1])) - current
    return next_one, next_two


def solution(mesh):
    banded = P("ka", None, "pa")
    return jax.shard_map(
        on_device,
        mesh=mesh,
        in_specs=(banded, banded, banded, P("ka", None, None), banded, P(None, "ka", "pa")),
        out_specs=(banded, banded),
        check_vma=False,
    )
```
